32 devices in a mesh: grp: 4 (over z), tile: 8 (over y, x, core).
Axes of the slice: x: 2, y: 2, z: 4, core: 2. Of those that a mesh axis runs over, the one named last changes fastest.
Arguments:
- node_feats: bfloat16 [2048, 1024], P(('grp', 'tile')), may hold values from -6 to 6
- feature_table: bfloat16 [32768, 1024], P(('grp', 'tile')), may hold values from -6 to 6
- nbr_ids: int32 [2048, 8], P(('grp', 'tile')), may hold values from 0 to 32767, as said below
- degree: int32 [2048], P(('grp', 'tile')), may hold values from 1 to 8
- weight_in: bfloat16 [2048, 4096], P(None, 'tile'), may hold values from -0.125 to 0.125
- bias_in: float32 [4096], P('tile'), may hold values from -3 to 3
- weight_out: bfloat16 [4096, 1024], P('tile'), may hold values from -0.125 to 0.125
- bias_out: float32 [1024], replicated, may hold values from -3 to 3
Outputs:
- embedding: bfloat16 [2048, 1024], P(('grp', 'tile'))
The draws below stay inside these ranges and needn't reach their ends.
Inputs may be any that keep to these rules, and one draw needn't show every extreme that they name: `nbr_ids`: table row r belongs to device r // 1024 in grp+tile order. Among the ids of the 64 nodes of one device, no owner device is named more than 32 times, and some owner exactly 32 times.
All inputs are finite; a program needn't handle non-finite values.
Results may differ from the reference program's by a relative error of at most 0.013.
Values may be sent and summed in bfloat16 or wider, within the bound.
A program may use at most 64 MiB of HBM per device.

```python
import jax
import jax.numpy as jnp
from jax import lax

FEAT = 1024
HIDDEN_SIZE = 4096
OUTW = 1024
NBR = 8
NODES_DEV = 64
TABLE_DEV = 1024
CAP = 32
NODES = 2048
TABLE_ROWS = 32768
N_GRP = 4
N_TILE = 8


def draw_nbr_ids(key, part):
    devices = N_GRP * N_TILE
    ref_count = NODES_DEV * NBR

    def one_device(dev_key):
        key_owner, key_shuffle, key_row = jax.random.split(dev_key, 3)
        owners = jax.random.permutation(key_owner, devices)
        shuffle = jax.random.permutation(key_shuffle, ref_count)
        owner_slot = jnp.arange(ref_count) // CAP
        chosen = owners[owner_slot][shuffle]
        row_ids = jax.random.randint(key_row, (ref_count,), 0, TABLE_DEV)
        return (chosen * TABLE_DEV + row_ids).reshape(NODES_DEV, NBR)
    dev_keys = jax.random.split(jax.random.fold_in(key, 17), devices)
    return jax.vmap(one_device)(dev_keys).reshape(NODES, NBR).astype(jnp.int32)


def set_ends(values, rng, least, top_value):
    extent = values.shape
    place = [jax.random.randint(jax.random.fold_in(rng, axis), (), 0, extent[axis]) for axis in range(len(extent))]
    values = values.at[tuple(place)].set(least)
    longest = extent.index(max(extent))
    place[longest] = (place[longest] + 1) % extent[longest]
    return values.at[tuple(place)].set(top_value)


def level_of(rng, dims, pieces, low, high):
    def one(axis_at, shards_of):
        steps = jax.random.uniform(jax.random.fold_in(jax.random.fold_in(rng, 6), axis_at), (shards_of,), jnp.float32, low / len(pieces), high / len(pieces))
        return jnp.repeat(jnp.exp(steps), dims[axis_at] // shards_of).reshape((-1,) + (1,) * (len(dims) - axis_at - 1))

    factor_of = one(*pieces[0])
    for cut in pieces[1:]:
        factor_of = factor_of * one(*cut)
    return factor_of


def scatter_about(key, dims, spread, most, pieces=(), kind=jnp.bfloat16):
    drawn = spread * jax.random.normal(key, dims, jnp.float32)
    if pieces:
        drawn = drawn * level_of(key, dims, pieces, -0.22, 0.18)
    return jnp.clip(drawn, -most, most).astype(kind)


def setup_inputs(seed: int = 0) -> dict:
    keys = jax.random.split(jax.random.key(seed), 9)
    node_feats = scatter_about(keys[0], (NODES, FEAT), 1.0, 6.0, ((0, 32),))
    feature_table = scatter_about(keys[1], (TABLE_ROWS, FEAT), 1.0, 6.0, ((0, 32),))
    nbr_ids = draw_nbr_ids(jax.random.fold_in(keys[8], 71), 0)
    degree = set_ends(jax.random.randint(keys[3], (NODES,), 1, NBR + 1), jax.random.fold_in(keys[3], 1), 1, NBR).astype(jnp.int32)
    weight_in = scatter_about(keys[4], (2 * FEAT, HIDDEN_SIZE), (2 * FEAT) ** -0.5, 0.125, ((1, 8),))
    bias_in = scatter_about(keys[5], (HIDDEN_SIZE,), 0.5, 3.0, ((0, 8),), jnp.float32)
    weight_out = scatter_about(keys[6], (HIDDEN_SIZE, OUTW), (HIDDEN_SIZE // 2) ** -0.5, 0.125, ((0, 8),))
    bias_out = scatter_about(keys[7], (OUTW,), 0.5, 3.0, (), jnp.float32)
    return dict(node_feats=node_feats, feature_table=feature_table, nbr_ids=nbr_ids, degree=degree, weight_in=weight_in, bias_in=bias_in, weight_out=weight_out, bias_out=bias_out)


def reference(node_feats, feature_table, nbr_ids, degree, weight_in, bias_in, weight_out, bias_out):
    summed = jnp.zeros((node_feats.shape[0], FEAT), jnp.float32)
    for column in range(NBR):
        fetched = jnp.take(feature_table, nbr_ids[:, column], axis=0).astype(jnp.float32)
        live_mask = (degree > column)[:, None]
        summed = summed + jnp.where(live_mask, fetched, jnp.float32(0.0))
    aggregate = (summed / degree.astype(jnp.float32)[:, None]).astype(jnp.bfloat16)
    joined = jnp.concatenate([node_feats, aggregate], axis=1)
    pre_act = jnp.dot(joined, weight_in, preferred_element_type=jnp.float32) + bias_in
    hidden = jax.nn.relu(pre_act).astype(jnp.bfloat16)
    block_width = HIDDEN_SIZE // N_TILE

    def add_block(running, block_index):
        begin = (block_index * block_width).astype(jnp.int32)
        hidden_block = lax.dynamic_slice_in_dim(hidden, begin, block_width, 1)
        weight_block = lax.dynamic_slice_in_dim(weight_out, begin, block_width, 0)
        partial_sum = jnp.dot(hidden_block, weight_block, preferred_element_type=jnp.float32).astype(jnp.bfloat16)
        partial_sum = lax.optimization_barrier(partial_sum)
        return running + partial_sum.astype(jnp.float32), None

    start_sum = jnp.zeros((node_feats.shape[0], OUTW), jnp.float32)
    running, unused = lax.scan(add_block, start_sum, jnp.arange(N_TILE))
    return (running + bias_out).astype(jnp.bfloat16)
```

```python
import functools

import jax
import jax.numpy as jnp
from jax import lax
from jax.experimental import pallas as pl
from jax.experimental.pallas import tpu as pltpu
from jax.sharding import PartitionSpec as P

MESH = pl.DeviceIdType.MESH
LANES = 128


def on_device_xla(node_feats, feature_table, nbr_ids, degree, weight_in, bias_in, weight_out, bias_out):
    group_count = lax.axis_size("grp")
    tile_count = lax.axis_size("tile")
    nodes_here, nbr_count = nbr_ids.shape
    rows_here, feat_width = feature_table.shape
    ref_count = nodes_here * nbr_count
    devices = group_count * tile_count
    slot_cap = max(2, 2 * ref_count // devices)
    ref_ids = nbr_ids.reshape(ref_count)
    owner_dev = ref_ids // rows_here
    local_row = ref_ids - owner_dev * rows_here
    same_owner = owner_dev[:, None] == owner_dev[None, :]
    positions = jnp.arange(ref_count)
    earlier_ref = positions[:, None] < positions[None, :]
    ref_rank = jnp.sum((same_owner & earlier_ref).astype(jnp.int32), axis=0)
    ref_slot = owner_dev * slot_cap + ref_rank
    wanted = jnp.zeros((devices * slot_cap,), jnp.int32).at[ref_slot].set(local_row)
    wanted = wanted.reshape(group_count, tile_count, slot_cap)
    asked_rows = lax.all_to_all(
        lax.all_to_all(wanted, "grp", split_axis=0, concat_axis=0, tiled=True),
        "tile",
        split_axis=1,
        concat_axis=1,
        tiled=True,
    )
    found_rows = jnp.take(feature_table, asked_rows.reshape(-1), axis=0)
    found_rows = found_rows.reshape(group_count, tile_count, slot_cap, feat_width)
    came_rows = lax.all_to_all(
        lax.all_to_all(found_rows, "grp", split_axis=0, concat_axis=0, tiled=True),
        "tile",
        split_axis=1,
        concat_axis=1,
        tiled=True,
    )
    arrived = came_rows.reshape(devices * slot_cap, feat_width)
    chosen = jnp.take(arrived, ref_slot, axis=0).reshape(nodes_here, nbr_count, feat_width)
    live_mask = (jnp.arange(nbr_count)[None, :] < degree[:, None]).astype(jnp.bfloat16)
    summed = jnp.einsum("nk,nkd->nd", live_mask, chosen, preferred_element_type=jnp.float32)
    aggregate = (summed / degree.astype(jnp.float32)[:, None]).astype(jnp.bfloat16)
    joined = jnp.concatenate([node_feats, aggregate], axis=1)
    pre_act = jnp.dot(
        lax.all_gather(joined, "tile", axis=0, tiled=True),
        weight_in,
        preferred_element_type=jnp.float32,
    )
    hidden = jax.nn.relu(pre_act + bias_in).astype(jnp.bfloat16)
    summed_out = lax.psum_scatter(
        jnp.dot(hidden, weight_out, preferred_element_type=jnp.float32).astype(jnp.bfloat16),
        "tile",
        scatter_dimension=0,
        tiled=True,
    ).astype(jnp.float32)
    return (summed_out + bias_out).astype(jnp.bfloat16)


def layer_kernel(
    groups,
    ids_ref, deg_ref, feats_hbm, table_hbm, win_hbm, bin_ref, wout_hbm, bout_ref,
    out_ref,
    table, win, wout, feats_own, idbuf, keys, rowkeys, count,
    sum_a, sum_b, rx, own_sum, zsend, zrecv, feats_all, agg_all, part, pouts, prx, qsend, qrx,
    ldsem, tsem, idsem_s, idsem_r, rs_s, rs_r, z_s, z_r, fg_s, fg_r, ag_s, ag_r, pp_s, pp_r, q_s, q_r,
):
    f32, bf16 = jnp.float32, jnp.bfloat16
    g = lax.axis_index("grp")
    t = lax.axis_index("tile")
    c = lax.rem(t, 2)
    x = lax.rem(t // 2, 2)
    y = t // 4
    rows, width = table_hbm.shape
    nodes = feats_hbm.shape[0]
    half = width // 2
    slots = ids_ref.shape[0]

    def dev(dg, rel, dc=0):
        xx = lax.rem(x + rel % 2, 2)
        yy = lax.rem(y + rel // 2, 2)
        cc = lax.rem(c + dc, 2)
        return (lax.rem(g + dg, groups), (yy * 2 + xx) * 2 + cc)

    def remote(src, dst, ss, rs, where):
        return pltpu.make_async_remote_copy(
            src_ref=src, dst_ref=dst, send_sem=ss, recv_sem=rs, device_id=where, device_id_type=MESH
        )

    mine = pl.ds(pl.multiple_of(c * rows, rows), rows)
    loads = [
        pltpu.make_async_copy(table_hbm, table.at[mine], ldsem.at[0]),
        pltpu.make_async_copy(feats_hbm, feats_all.at[0, 0], ldsem.at[1]),
        pltpu.make_async_copy(win_hbm, win, ldsem.at[2]),
        pltpu.make_async_copy(wout_hbm, wout, ldsem.at[3]),
        pltpu.make_async_copy(feats_hbm, feats_own, ldsem.at[4]),
    ]
    for load in loads:
        load.start()

    barrier = pltpu.get_barrier_semaphore()
    peers = [dev(dg, rel) for dg in range(groups) for rel in range(4) if dg or rel]
    peers.append(dev(0, 0, 1))
    for where in peers:
        pl.semaphore_signal(barrier, inc=1, device_id=where, device_id_type=MESH)

    lane = lax.broadcasted_iota(jnp.int32, (16, 2 * rows), 1)
    rowkeys[...] = jnp.left_shift(lax.rem(lane, LANES) + LANES, lane // LANES).astype(f32).astype(bf16)
    idbuf[groups - 1, 0] = ids_ref[...]

    pl.semaphore_wait(barrier, len(peers))

    id_sends = []
    for i in range(groups):
        for rel in range(4):
            if i == groups - 1 and rel == 0:
                continue
            send = remote(ids_ref, idbuf.at[i, rel], idsem_s.at[i, rel], idsem_r.at[i, rel],
                          dev(groups - 1 - i, rel))
            send.start()
            id_sends.append(send)
    tsend = remote(table_hbm, table.at[mine], tsem.at[0], tsem.at[1], dev(0, 0, 1))
    tsend.start()
    loads[4].wait()
    fsends = []
    for rel in (3, 1, 2):
        send = remote(feats_own, feats_all.at[0, rel], fg_s.at[0, rel], fg_r.at[0, rel], dev(0, rel))
        send.start()
        fsends.append(send)
    send = remote(feats_own, feats_all.at[1, 0], fg_s.at[1, 0], fg_r.at[1, 0], dev(0, 0, 1))
    send.start()
    fsends.append(send)

    for send in id_sends:
        send.wait_recv()
    base = (g * lax.axis_size("tile") + (y * 2 + x) * 2) * rows
    local = idbuf[...].reshape(groups * 4 * slots, LANES) - base
    inside = (local >= 0) & (local < 2 * rows)
    safe = jnp.where(inside, local, 0)
    key = jnp.left_shift(lax.rem(safe, LANES) + LANES, safe // LANES)
    keyf = jnp.where(inside, key, 0).astype(f32)
    if keyf.shape[0] < LANES:
        keyf = jnp.concatenate([keyf, jnp.zeros((LANES - keyf.shape[0], LANES), f32)], axis=0)
    keys[...] = keyf.T

    loads[0].wait()
    tsend.wait_recv()

    def rs_copy(kind, i):
        src = (sum_a.at[i, 3], sum_a.at[i, 1], sum_b.at[i, 3], sum_b.at[i, 2],
               sum_a.at[i, 2], sum_b.at[i, 1])[kind]
        return remote(src, rx.at[kind, i], rs_s.at[kind, i], rs_r.at[kind, i],
                      dev(0, (1, 1, 2, 2, 2, 1)[kind]))

    one = jnp.ones((16, 2 * rows), bf16)
    zero = jnp.zeros((16, 2 * rows), bf16)

    def make_sums(i):
        for rel in range(4):
            block = i * 4 + rel

            def group(r, carry, rel=rel, block=block):
                at = pl.ds(pl.multiple_of(r * 16, 16), 16)
                kk = keys[at, :]
                rk = rowkeys[...]
                total = zero
                for k in range(slots):
                    col = block * slots + k
                    wide = jnp.broadcast_to(kk[:, col:col + 1], (16, LANES)).astype(bf16)
                    wide = jnp.concatenate([wide] * (2 * rows // LANES), axis=1)
                    total = total + jnp.where(wide == rk, one, zero)
                count[pl.ds(pl.multiple_of(rel * nodes + r * 16, 16), 16), :] = total
                return carry

            lax.fori_loop(0, nodes // 16, group, 0)
        step = min(256, half)
        for n0 in range(0, width, step):
            got = jnp.dot(count[...], table[:, n0:n0 + step], preferred_element_type=f32).astype(bf16)
            into, at = (sum_a, n0) if n0 < half else (sum_b, n0 - half)
            into[i, :, :, at:at + step] = got.reshape(4, nodes, step)
        for kind in (0, 2, 1, 3):
            rs_copy(kind, i).start()

    def pass_on(i):
        rs_copy(0, i).wait_recv()
        sum_a[i, 2] = (sum_a[i, 2].astype(f32) + rx[0, i].astype(f32)).astype(bf16)
        rs_copy(4, i).start()
        rs_copy(2, i).wait_recv()
        sum_b[i, 1] = (sum_b[i, 1].astype(f32) + rx[2, i].astype(f32)).astype(bf16)
        rs_copy(5, i).start()

    def z_copy(i):
        return remote(zsend.at[i], zrecv.at[i], z_s.at[i], z_r.at[i], dev(i + 1, 0))

    def plane_sum(i):
        for kind in (1, 4, 3, 5):
            rs_copy(kind, i).wait_recv()
        a = sum_a[i, 0].astype(f32) + rx[1, i].astype(f32) + rx[4, i].astype(f32)
        b = sum_b[i, 0].astype(f32) + rx[3, i].astype(f32) + rx[5, i].astype(f32)
        if i < groups - 1:
            zsend[i, :, 0:half] = a.astype(bf16)
            zsend[i, :, half:width] = b.astype(bf16)
            z_copy(i).start()
        else:
            own_sum[:, 0:half] = a
            own_sum[:, half:width] = b

    def gather_copy(buf, ss, rs, kind, rel):
        if kind == 0:
            return remote(buf.at[0, 0], buf.at[0, rel], ss.at[0, rel], rs.at[0, rel], dev(0, rel))
        return remote(buf.at[0, rel], buf.at[1, rel], ss.at[1, rel], rs.at[1, rel], dev(0, 0, 1))

    make_sums(0)
    make_sums(1)
    loads[1].wait()
    for rel in (1, 2, 3):
        gather_copy(feats_all, fg_s, fg_r, 0, rel).wait_recv()
        gather_copy(feats_all, fg_s, fg_r, 1, rel).start()
    pass_on(0)
    for i in range(2, groups):
        make_sums(i)
        pass_on(i - 1)
        plane_sum(i - 2)

    loads[2].wait()
    for rel in range(4):
        gather_copy(feats_all, fg_s, fg_r, 1, rel).wait_recv()
    hid = win.shape[1]

    part[...] = jnp.dot(
        feats_all[...].reshape(8 * nodes, width), win[0:width, :], preferred_element_type=f32
    ).reshape(2, 4, nodes, hid) + bin_ref[...].reshape(1, 1, 1, hid)

    plane_sum(groups - 2)
    pass_on(groups - 1)
    plane_sum(groups - 1)

    total = own_sum[...]
    for i in range(groups - 1):
        z_copy(i).wait_recv()
        total = total + zrecv[i].astype(f32)
    agg_all[0, 0] = (total / deg_ref[...]).astype(bf16)
    for rel in (3, 1, 2):
        gather_copy(agg_all, ag_s, ag_r, 0, rel).start()
    gather_copy(agg_all, ag_s, ag_r, 1, 0).start()
    loads[3].wait()

    def p_copy(rel):
        return remote(pouts.at[1, rel], prx.at[rel], pp_s.at[rel], pp_r.at[rel], dev(0, 0, 1))

    def q_copy(rel):
        return remote(qsend.at[rel - 1], qrx.at[rel - 1], q_s.at[rel - 1], q_r.at[rel - 1], dev(0, rel))

    for rel in (1, 2, 3):
        gather_copy(agg_all, ag_s, ag_r, 0, rel).wait_recv()
        gather_copy(agg_all, ag_s, ag_r, 1, rel).start()
    for rel in range(4):
        gather_copy(agg_all, ag_s, ag_r, 1, rel).wait_recv()
        both = agg_all[:, rel].reshape(2 * nodes, width)
        pre = jnp.dot(both, win[width:2 * width, :], preferred_element_type=f32)
        pre = pre + part[:, rel].reshape(2 * nodes, hid)
        hidden = jnp.maximum(pre, 0.0).astype(bf16)
        got = jnp.dot(hidden, wout[...], preferred_element_type=f32).astype(bf16)
        pouts[:, rel] = got.reshape(2, nodes, got.shape[1])
        p_copy(rel).start()
    for rel in (3, 1, 2):
        p_copy(rel).wait_recv()
        qsend[rel - 1] = (pouts[0, rel].astype(f32) + prx[rel].astype(f32)).astype(bf16)
        q_copy(rel).start()
    p_copy(0).wait_recv()
    final = pouts[0, 0].astype(f32) + prx[0].astype(f32) + bout_ref[...]
    for rel in (1, 2, 3):
        q_copy(rel).wait_recv()
        final = final + qrx[rel - 1].astype(f32)
    out_ref[...] = final.astype(bf16)

    for send in id_sends + fsends:
        send.wait_send()
    tsend.wait_send()
    for rel in (1, 2, 3):
        gather_copy(feats_all, fg_s, fg_r, 1, rel).wait_send()
        gather_copy(agg_all, ag_s, ag_r, 0, rel).wait_send()
        q_copy(rel).wait_send()
    for rel in range(4):
        gather_copy(agg_all, ag_s, ag_r, 1, rel).wait_send()
        p_copy(rel).wait_send()
    for i in range(groups):
        for kind in range(6):
            rs_copy(kind, i).wait_send()
        if i < groups - 1:
            z_copy(i).wait_send()


def on_device_fused(groups, node_feats, feature_table, nbr_ids, degree, weight_in, bias_in, weight_out, bias_out):
    nodes, slots = nbr_ids.shape
    rows, width = feature_table.shape
    hid = weight_in.shape[1]
    outw = weight_out.shape[1]
    bf16, f32 = jnp.bfloat16, jnp.float32
    live = jnp.arange(slots, dtype=jnp.int32)[:, None] < degree[None, :]
    ids = jnp.pad(jnp.where(live, nbr_ids.T, -1), ((0, 0), (0, LANES - nodes)), constant_values=-1)
    vmem = pl.BlockSpec(memory_space=pltpu.VMEM)
    hbm = pl.BlockSpec(memory_space=pl.ANY)
    half = width // 2
    dma = pltpu.SemaphoreType.DMA
    return pl.pallas_call(
        functools.partial(layer_kernel, groups),
        out_shape=jax.ShapeDtypeStruct((nodes, outw), bf16),
        in_specs=[vmem, vmem, hbm, hbm, hbm, vmem, hbm, vmem],
        out_specs=vmem,
        scratch_shapes=[
            pltpu.VMEM((2 * rows, width), bf16),
            pltpu.VMEM((2 * width, hid), bf16),
            pltpu.VMEM((hid, outw), bf16),
            pltpu.VMEM((nodes, width), bf16),
            pltpu.VMEM((groups, 4, slots, LANES), jnp.int32),
            pltpu.VMEM((LANES, LANES), f32),
            pltpu.VMEM((16, 2 * rows), bf16),
            pltpu.VMEM((4 * nodes, 2 * rows), bf16),
            pltpu.VMEM((groups, 4, nodes, half), bf16),
            pltpu.VMEM((groups, 4, nodes, half), bf16),
            pltpu.VMEM((6, groups, nodes, half), bf16),
            pltpu.VMEM((nodes, width), f32),
            pltpu.VMEM((groups - 1, nodes, width), bf16),
            pltpu.VMEM((groups - 1, nodes, width), bf16),
            pltpu.VMEM((2, 4, nodes, width), bf16),
            pltpu.VMEM((2, 4, nodes, width), bf16),
            pltpu.VMEM((2, 4, nodes, hid), f32),
            pltpu.VMEM((2, 4, nodes, outw), bf16),
            pltpu.VMEM((4, nodes, outw), bf16),
            pltpu.VMEM((3, nodes, outw), bf16),
            pltpu.VMEM((3, nodes, outw), bf16),
            dma((5,)), dma((2,)),
            dma((groups, 4)), dma((groups, 4)),
            dma((6, groups)), dma((6, groups)),
            dma((groups - 1,)), dma((groups - 1,)),
            dma((2, 4)), dma((2, 4)),
            dma((2, 4)), dma((2, 4)),
            dma((4,)), dma((4,)),
            dma((3,)), dma((3,)),
        ],
        compiler_params=pltpu.CompilerParams(
            collective_id=0, has_side_effects=True, vmem_limit_bytes=48 * 1024 * 1024
        ),
    )(
        ids, degree.astype(f32)[:, None], node_feats, feature_table, weight_in,
        bias_in[None, :], weight_out, bias_out[None, :],
    )


def solution(mesh):
    groups, tiles = mesh.shape["grp"], mesh.shape["tile"]

    def on_device(node_feats, feature_table, nbr_ids, degree, *weights):
        nodes, slots = nbr_ids.shape
        rows, width = feature_table.shape
        fits = (
            tiles == 8
            and groups > 2
            and groups * 4 * slots <= LANES
            and nodes <= LANES
            and nodes % 16 == 0
            and rows % LANES == 0
            and 2 * rows // LANES <= 16
            and width % (4 * LANES) == 0
        )
        if fits:
            return on_device_fused(groups, node_feats, feature_table, nbr_ids, degree, *weights)
        return on_device_xla(node_feats, feature_table, nbr_ids, degree, *weights)

    return jax.shard_map(
        on_device,
        mesh=mesh,
        in_specs=(
            P(("grp", "tile"), None),
            P(("grp", "tile"), None),
            P(("grp", "tile"), None),
            P(("grp", "tile")),
            P(None, "tile"),
            P("tile"),
            P("tile", None),
            P(),
        ),
        out_specs=P(("grp", "tile"), None),
        check_vma=False,
    )
```

```python
import functools

import jax
import jax.numpy as jnp
from jax import lax
from jax.experimental import pallas as pl
from jax.experimental.pallas import tpu as pltpu
from jax.sharding import PartitionSpec as P

MESH = pl.DeviceIdType.MESH
LANES = 128


def on_device_xla(node_feats, feature_table, nbr_ids, degree, weight_in, bias_in, weight_out, bias_out):
    group_count = lax.axis_size("grp")
    tile_count = lax.axis_size("tile")
    nodes_here, nbr_count = nbr_ids.shape
    rows_here, feat_width = feature_table.shape
    ref_count = nodes_here * nbr_count
    devices = group_count * tile_count
    slot_cap = max(2, 2 * ref_count // devices)
    ref_ids = nbr_ids.reshape(ref_count)
    owner_dev = ref_ids // rows_here
    local_row = ref_ids - owner_dev * rows_here
    same_owner = owner_dev[:, None] == owner_dev[None, :]
    positions = jnp.arange(ref_count)
    earlier_ref = positions[:, None] < positions[None, :]
    ref_rank = jnp.sum((same_owner & earlier_ref).astype(jnp.int32), axis=0)
    ref_slot = owner_dev * slot_cap + ref_rank
    wanted = jnp.zeros((devices * slot_cap,), jnp.int32).at[ref_slot].set(local_row)
    wanted = wanted.reshape(group_count, tile_count, slot_cap)
    asked_rows = lax.all_to_all(
        lax.all_to_all(wanted, "grp", split_axis=0, concat_axis=0, tiled=True),
        "tile",
        split_axis=1,
        concat_axis=1,
        tiled=True,
    )
    found_rows = jnp.take(feature_table, asked_rows.reshape(-1), axis=0)
    found_rows = found_rows.reshape(group_count, tile_count, slot_cap, feat_width)
    came_rows = lax.all_to_all(
        lax.all_to_all(found_rows, "grp", split_axis=0, concat_axis=0, tiled=True),
        "tile",
        split_axis=1,
        concat_axis=1,
        tiled=True,
    )
    arrived = came_rows.reshape(devices * slot_cap, feat_width)
    chosen = jnp.take(arrived, ref_slot, axis=0).reshape(nodes_here, nbr_count, feat_width)
    live_mask = (jnp.arange(nbr_count)[None, :] < degree[:, None]).astype(jnp.bfloat16)
    summed = jnp.einsum("nk,nkd->nd", live_mask, chosen, preferred_element_type=jnp.float32)
    aggregate = (summed / degree.astype(jnp.float32)[:, None]).astype(jnp.bfloat16)
    joined = jnp.concatenate([node_feats, aggregate], axis=1)
    pre_act = jnp.dot(
        lax.all_gather(joined, "tile", axis=0, tiled=True),
        weight_in,
        preferred_element_type=jnp.float32,
    )
    hidden = jax.nn.relu(pre_act + bias_in).astype(jnp.bfloat16)
    summed_out = lax.psum_scatter(
        jnp.dot(hidden, weight_out, preferred_element_type=jnp.float32).astype(jnp.bfloat16),
        "tile",
        scatter_dimension=0,
        tiled=True,
    ).astype(jnp.float32)
    return (summed_out + bias_out).astype(jnp.bfloat16)


def layer_kernel(
    groups,
    ids_hbm, deg_hbm, feats_hbm, table_hbm, win_hbm, bin_hbm, wout_hbm, bout_hbm,
    out_ref,
    ids_raw, deg_raw, bin_ref, bout_ref, ids_ref, deg_row, deg_col,
    table, win, wout, feats_own, idbuf, keys, rowkeys, count,
    sum_a, sum_b, rx, own_sum, zsend, zrecv, feats_all, agg_all, part, pouts, prx, qsend, qrx,
    ldsem, tsem, idsem_s, idsem_r, rs_s, rs_r, z_s, z_r, fg_s, fg_r, ag_s, ag_r, pp_s, pp_r, q_s, q_r,
):
    f32, bf16 = jnp.float32, jnp.bfloat16
    g = lax.axis_index("grp")
    t = lax.axis_index("tile")
    c = lax.rem(t, 2)
    x = lax.rem(t // 2, 2)
    y = t // 4
    rows, width = table_hbm.shape
    nodes = feats_hbm.shape[0]
    half = width // 2
    slots = ids_hbm.shape[0]

    def dev(dg, rel, dc=0):
        xx = lax.rem(x + rel % 2, 2)
        yy = lax.rem(y + rel // 2, 2)
        cc = lax.rem(c + dc, 2)
        return (lax.rem(g + dg, groups), (yy * 2 + xx) * 2 + cc)

    def remote(src, dst, ss, rs, where):
        return pltpu.make_async_remote_copy(
            src_ref=src, dst_ref=dst, send_sem=ss, recv_sem=rs, device_id=where, device_id_type=MESH
        )

    mine = pl.ds(pl.multiple_of(c * rows, rows), rows)
    loads = [
        pltpu.make_async_copy(table_hbm, table.at[mine], ldsem.at[0]),
        pltpu.make_async_copy(feats_hbm, feats_all.at[0, 0], ldsem.at[1]),
        pltpu.make_async_copy(win_hbm, win, ldsem.at[2]),
        pltpu.make_async_copy(wout_hbm, wout, ldsem.at[3]),
        pltpu.make_async_copy(feats_hbm, feats_own, ldsem.at[4]),
        pltpu.make_async_copy(ids_hbm, ids_raw, ldsem.at[5]),
        pltpu.make_async_copy(deg_hbm, deg_raw, ldsem.at[6]),
        pltpu.make_async_copy(bin_hbm, bin_ref, ldsem.at[7]),
        pltpu.make_async_copy(bout_hbm, bout_ref, ldsem.at[8]),
    ]
    for at in (5, 6, 4, 0, 1, 2, 7, 3, 8):
        loads[at].start()

    barrier = pltpu.get_barrier_semaphore()
    peers = [dev(dg, rel) for dg in range(groups) for rel in range(4) if dg or rel]
    peers.append(dev(0, 0, 1))
    for where in peers:
        pl.semaphore_signal(barrier, inc=1, device_id=where, device_id_type=MESH)

    lane = lax.broadcasted_iota(jnp.int32, (16, 2 * rows), 1)
    rowkeys[...] = jnp.left_shift(lax.rem(lane, LANES) + LANES, lane // LANES).astype(f32).astype(bf16)
    loads[5].wait()
    loads[6].wait()
    degree = deg_raw[...]
    live = lax.broadcasted_iota(jnp.int32, (slots, nodes), 0) < degree
    if nodes < LANES:
        ids_ref[...] = jnp.full((slots, LANES), -1, jnp.int32)
    ids_ref[:, 0:nodes] = jnp.where(live, ids_raw[...], -1)
    idbuf[groups - 1, 0] = ids_ref[...]
    deg_row[...] = jnp.ones((1, LANES), f32)
    deg_row[:, 0:nodes] = degree.astype(f32)

    pl.semaphore_wait(barrier, len(peers))

    id_sends = []
    for i in range(groups):
        for rel in range(4):
            if i == groups - 1 and rel == 0:
                continue
            send = remote(ids_ref, idbuf.at[i, rel], idsem_s.at[i, rel], idsem_r.at[i, rel],
                          dev(groups - 1 - i, rel))
            send.start()
            id_sends.append(send)
    tsend = remote(table_hbm, table.at[mine], tsem.at[0], tsem.at[1], dev(0, 0, 1))
    tsend.start()
    loads[4].wait()
    fsends = []
    for rel in (3, 1, 2):
        send = remote(feats_own, feats_all.at[0, rel], fg_s.at[0, rel], fg_r.at[0, rel], dev(0, rel))
        send.start()
        fsends.append(send)
    send = remote(feats_own, feats_all.at[1, 0], fg_s.at[1, 0], fg_r.at[1, 0], dev(0, 0, 1))
    send.start()
    fsends.append(send)

    deg_col[...] = jnp.broadcast_to(deg_row[...], (LANES, LANES)).T
    for send in id_sends:
        send.wait_recv()
    base = (g * lax.axis_size("tile") + (y * 2 + x) * 2) * rows
    local = idbuf[...].reshape(groups * 4 * slots, LANES) - base
    inside = (local >= 0) & (local < 2 * rows)
    safe = jnp.where(inside, local, 0)
    key = jnp.left_shift(lax.rem(safe, LANES) + LANES, safe // LANES)
    keyf = jnp.where(inside, key, 0).astype(f32)
    if keyf.shape[0] < LANES:
        keyf = jnp.concatenate([keyf, jnp.zeros((LANES - keyf.shape[0], LANES), f32)], axis=0)
    keys[...] = keyf.T

    loads[0].wait()
    tsend.wait_recv()

    def rs_copy(kind, i):
        src = (sum_a.at[i, 3], sum_a.at[i, 1], sum_b.at[i, 3], sum_b.at[i, 2],
               sum_a.at[i, 2], sum_b.at[i, 1])[kind]
        return remote(src, rx.at[kind, i], rs_s.at[kind, i], rs_r.at[kind, i],
                      dev(0, (1, 1, 2, 2, 2, 1)[kind]))

    one = jnp.ones((16, 2 * rows), bf16)
    zero = jnp.zeros((16, 2 * rows), bf16)

    def make_sums(i):
        for rel in range(4):
            block = i * 4 + rel

            def group(r, carry, rel=rel, block=block):
                at = pl.ds(pl.multiple_of(r * 16, 16), 16)
                kk = keys[at, :]
                rk = rowkeys[...]
                total = zero
                for k in range(slots):
                    col = block * slots + k
                    wide = jnp.broadcast_to(kk[:, col:col + 1], (16, LANES)).astype(bf16)
                    wide = jnp.concatenate([wide] * (2 * rows // LANES), axis=1)
                    total = total + jnp.where(wide == rk, one, zero)
                count[pl.ds(pl.multiple_of(rel * nodes + r * 16, 16), 16), :] = total
                return carry

            lax.fori_loop(0, nodes // 16, group, 0)
        step = min(256, half)
        for n0 in range(0, width, step):
            got = jnp.dot(count[...], table[:, n0:n0 + step], preferred_element_type=f32).astype(bf16)
            into, at = (sum_a, n0) if n0 < half else (sum_b, n0 - half)
            into[i, :, :, at:at + step] = got.reshape(4, nodes, step)
        for kind in (0, 2, 1, 3):
            rs_copy(kind, i).start()

    def pass_on(i):
        rs_copy(0, i).wait_recv()
        sum_a[i, 2] = (sum_a[i, 2].astype(f32) + rx[0, i].astype(f32)).astype(bf16)
        rs_copy(4, i).start()
        rs_copy(2, i).wait_recv()
        sum_b[i, 1] = (sum_b[i, 1].astype(f32) + rx[2, i].astype(f32)).astype(bf16)
        rs_copy(5, i).start()

    def z_copy(i):
        return remote(zsend.at[i], zrecv.at[i], z_s.at[i], z_r.at[i], dev(i + 1, 0))

    def plane_sum(i):
        for kind in (1, 4, 3, 5):
            rs_copy(kind, i).wait_recv()
        a = sum_a[i, 0].astype(f32) + rx[1, i].astype(f32) + rx[4, i].astype(f32)
        b = sum_b[i, 0].astype(f32) + rx[3, i].astype(f32) + rx[5, i].astype(f32)
        if i < groups - 1:
            zsend[i, :, 0:half] = a.astype(bf16)
            zsend[i, :, half:width] = b.astype(bf16)
            z_copy(i).start()
        else:
            own_sum[:, 0:half] = a
            own_sum[:, half:width] = b

    def gather_copy(buf, ss, rs, kind, rel):
        if kind == 0:
            return remote(buf.at[0, 0], buf.at[0, rel], ss.at[0, rel], rs.at[0, rel], dev(0, rel))
        return remote(buf.at[0, rel], buf.at[1, rel], ss.at[1, rel], rs.at[1, rel], dev(0, 0, 1))

    make_sums(0)
    make_sums(1)
    loads[1].wait()
    for rel in (1, 2, 3):
        gather_copy(feats_all, fg_s, fg_r, 0, rel).wait_recv()
        gather_copy(feats_all, fg_s, fg_r, 1, rel).start()
    pass_on(0)
    for i in range(2, groups):
        make_sums(i)
        pass_on(i - 1)
        plane_sum(i - 2)

    loads[2].wait()
    loads[7].wait()
    for rel in range(4):
        gather_copy(feats_all, fg_s, fg_r, 1, rel).wait_recv()
    hid = win.shape[1]

    part[...] = jnp.dot(
        feats_all[...].reshape(8 * nodes, width), win[0:width, :], preferred_element_type=f32
    ).reshape(2, 4, nodes, hid) + bin_ref[...].reshape(1, 1, 1, hid)

    plane_sum(groups - 2)
    pass_on(groups - 1)
    plane_sum(groups - 1)

    total = own_sum[...]
    for i in range(groups - 1):
        z_copy(i).wait_recv()
        total = total + zrecv[i].astype(f32)
    divisor = jnp.concatenate([deg_col[0:nodes, :]] * (width // LANES), axis=1)
    agg_all[0, 0] = (total / divisor).astype(bf16)
    for rel in (3, 1, 2):
        gather_copy(agg_all, ag_s, ag_r, 0, rel).start()
    gather_copy(agg_all, ag_s, ag_r, 1, 0).start()
    loads[3].wait()
    loads[8].wait()

    def p_copy(rel):
        return remote(pouts.at[1, rel], prx.at[rel], pp_s.at[rel], pp_r.at[rel], dev(0, 0, 1))

    def q_copy(rel):
        return remote(qsend.at[rel - 1], qrx.at[rel - 1], q_s.at[rel - 1], q_r.at[rel - 1], dev(0, rel))

    def forward(rel):
        gather_copy(agg_all, ag_s, ag_r, 0, rel).wait_recv()
        gather_copy(agg_all, ag_s, ag_r, 1, rel).start()

    def block(rel):
        gather_copy(agg_all, ag_s, ag_r, 1, rel).wait_recv()
        both = agg_all[:, rel].reshape(2 * nodes, width)
        pre = jnp.dot(both, win[width:2 * width, :], preferred_element_type=f32)
        pre = pre + part[:, rel].reshape(2 * nodes, hid)
        hidden = jnp.maximum(pre, 0.0).astype(bf16)
        got = jnp.dot(hidden, wout[...], preferred_element_type=f32).astype(bf16)
        pouts[:, rel] = got.reshape(2, nodes, got.shape[1])
        p_copy(rel).start()

    def send_out(rel):
        p_copy(rel).wait_recv()
        qsend[rel - 1] = (pouts[0, rel].astype(f32) + prx[rel].astype(f32)).astype(bf16)
        q_copy(rel).start()

    block(0)
    forward(1)
    forward(2)
    block(1)
    forward(3)
    block(2)
    send_out(1)
    block(3)
    send_out(2)
    send_out(3)
    p_copy(0).wait_recv()
    final = pouts[0, 0].astype(f32) + prx[0].astype(f32) + bout_ref[...]
    for rel in (1, 2, 3):
        q_copy(rel).wait_recv()
        final = final + qrx[rel - 1].astype(f32)
    out_ref[...] = final.astype(bf16)

    for send in id_sends + fsends:
        send.wait_send()
    tsend.wait_send()
    for rel in (1, 2, 3):
        gather_copy(feats_all, fg_s, fg_r, 1, rel).wait_send()
        gather_copy(agg_all, ag_s, ag_r, 0, rel).wait_send()
        q_copy(rel).wait_send()
    for rel in range(4):
        gather_copy(agg_all, ag_s, ag_r, 1, rel).wait_send()
        p_copy(rel).wait_send()
    for i in range(groups):
        for kind in range(6):
            rs_copy(kind, i).wait_send()
        if i < groups - 1:
            z_copy(i).wait_send()


def on_device_fused(groups, node_feats, feature_table, nbr_ids, degree, weight_in, bias_in, weight_out, bias_out):
    nodes, slots = nbr_ids.shape
    rows, width = feature_table.shape
    hid = weight_in.shape[1]
    outw = weight_out.shape[1]
    bf16, f32 = jnp.bfloat16, jnp.float32
    vmem = pl.BlockSpec(memory_space=pltpu.VMEM)
    hbm = pl.BlockSpec(memory_space=pltpu.HBM)
    half = width // 2
    dma = pltpu.SemaphoreType.DMA
    return pl.pallas_call(
        functools.partial(layer_kernel, groups),
        out_shape=jax.ShapeDtypeStruct((nodes, outw), bf16),
        in_specs=[hbm] * 8,
        out_specs=vmem,
        scratch_shapes=[
            pltpu.VMEM((slots, nodes), jnp.int32),
            pltpu.VMEM((1, nodes), jnp.int32),
            pltpu.VMEM((1, hid), f32),
            pltpu.VMEM((1, outw), f32),
            pltpu.VMEM((slots, LANES), jnp.int32),
            pltpu.VMEM((1, LANES), f32),
            pltpu.VMEM((LANES, LANES), f32),
            pltpu.VMEM((2 * rows, width), bf16),
            pltpu.VMEM((2 * width, hid), bf16),
            pltpu.VMEM((hid, outw), bf16),
            pltpu.VMEM((nodes, width), bf16),
            pltpu.VMEM((groups, 4, slots, LANES), jnp.int32),
            pltpu.VMEM((LANES, LANES), f32),
            pltpu.VMEM((16, 2 * rows), bf16),
            pltpu.VMEM((4 * nodes, 2 * rows), bf16),
            pltpu.VMEM((groups, 4, nodes, half), bf16),
            pltpu.VMEM((groups, 4, nodes, half), bf16),
            pltpu.VMEM((6, groups, nodes, half), bf16),
            pltpu.VMEM((nodes, width), f32),
            pltpu.VMEM((groups - 1, nodes, width), bf16),
            pltpu.VMEM((groups - 1, nodes, width), bf16),
            pltpu.VMEM((2, 4, nodes, width), bf16),
            pltpu.VMEM((2, 4, nodes, width), bf16),
            pltpu.VMEM((2, 4, nodes, hid), f32),
            pltpu.VMEM((2, 4, nodes, outw), bf16),
            pltpu.VMEM((4, nodes, outw), bf16),
            pltpu.VMEM((3, nodes, outw), bf16),
            pltpu.VMEM((3, nodes, outw), bf16),
            dma((9,)), dma((2,)),
            dma((groups, 4)), dma((groups, 4)),
            dma((6, groups)), dma((6, groups)),
            dma((groups - 1,)), dma((groups - 1,)),
            dma((2, 4)), dma((2, 4)),
            dma((2, 4)), dma((2, 4)),
            dma((4,)), dma((4,)),
            dma((3,)), dma((3,)),
        ],
        compiler_params=pltpu.CompilerParams(
            collective_id=0, has_side_effects=True, vmem_limit_bytes=67043328
        ),
    )(
        nbr_ids.T, degree[None, :], node_feats, feature_table, weight_in,
        bias_in[None, :], weight_out, bias_out[None, :],
    )


def solution(mesh):
    groups, tiles = mesh.shape["grp"], mesh.shape["tile"]

    def on_device(node_feats, feature_table, nbr_ids, degree, *weights):
        nodes, slots = nbr_ids.shape
        rows, width = feature_table.shape
        fits = (
            tiles == 8
            and groups > 2
            and groups * 4 * slots <= LANES
            and nodes <= LANES
            and nodes % 16 == 0
            and rows % LANES == 0
            and 2 * rows // LANES <= 16
            and width % (4 * LANES) == 0
        )
        if fits:
            return on_device_fused(groups, node_feats, feature_table, nbr_ids, degree, *weights)
        return on_device_xla(node_feats, feature_table, nbr_ids, degree, *weights)

    return jax.shard_map(
        on_device,
        mesh=mesh,
        in_specs=(
            P(("grp", "tile"), None),
            P(("grp", "tile"), None),
            P(("grp", "tile"), None),
            P(("grp", "tile")),
            P(None, "tile"),
            P("tile"),
            P("tile", None),
            P(),
        ),
        out_specs=P(("grp", "tile"), None),
        check_vma=False,
    )
```

```python
import functools

import jax
import jax.numpy as jnp
from jax import lax
from jax.experimental import pallas as pl
from jax.experimental.pallas import tpu as pltpu
from jax.sharding import PartitionSpec as P

MESH = pl.DeviceIdType.MESH
LANES = 128


def on_device_xla(node_feats, feature_table, nbr_ids, degree, weight_in, bias_in, weight_out, bias_out):
    group_count = lax.axis_size("grp")
    tile_count = lax.axis_size("tile")
    nodes_here, nbr_count = nbr_ids.shape
    rows_here, feat_width = feature_table.shape
    ref_count = nodes_here * nbr_count
    devices = group_count * tile_count
    slot_cap = max(2, 2 * ref_count // devices)
    ref_ids = nbr_ids.reshape(ref_count)
    owner_dev = ref_ids // rows_here
    local_row = ref_ids - owner_dev * rows_here
    same_owner = owner_dev[:, None] == owner_dev[None, :]
    positions = jnp.arange(ref_count)
    earlier_ref = positions[:, None] < positions[None, :]
    ref_rank = jnp.sum((same_owner & earlier_ref).astype(jnp.int32), axis=0)
    ref_slot = owner_dev * slot_cap + ref_rank
    wanted = jnp.zeros((devices * slot_cap,), jnp.int32).at[ref_slot].set(local_row)
    wanted = wanted.reshape(group_count, tile_count, slot_cap)
    asked_rows = lax.all_to_all(
        lax.all_to_all(wanted, "grp", split_axis=0, concat_axis=0, tiled=True),
        "tile",
        split_axis=1,
        concat_axis=1,
        tiled=True,
    )
    found_rows = jnp.take(feature_table, asked_rows.reshape(-1), axis=0)
    found_rows = found_rows.reshape(group_count, tile_count, slot_cap, feat_width)
    came_rows = lax.all_to_all(
        lax.all_to_all(found_rows, "grp", split_axis=0, concat_axis=0, tiled=True),
        "tile",
        split_axis=1,
        concat_axis=1,
        tiled=True,
    )
    arrived = came_rows.reshape(devices * slot_cap, feat_width)
    chosen = jnp.take(arrived, ref_slot, axis=0).reshape(nodes_here, nbr_count, feat_width)
    live_mask = (jnp.arange(nbr_count)[None, :] < degree[:, None]).astype(jnp.bfloat16)
    summed = jnp.einsum("nk,nkd->nd", live_mask, chosen, preferred_element_type=jnp.float32)
    aggregate = (summed / degree.astype(jnp.float32)[:, None]).astype(jnp.bfloat16)
    joined = jnp.concatenate([node_feats, aggregate], axis=1)
    pre_act = jnp.dot(
        lax.all_gather(joined, "tile", axis=0, tiled=True),
        weight_in,
        preferred_element_type=jnp.float32,
    )
    hidden = jax.nn.relu(pre_act + bias_in).astype(jnp.bfloat16)
    summed_out = lax.psum_scatter(
        jnp.dot(hidden, weight_out, preferred_element_type=jnp.float32).astype(jnp.bfloat16),
        "tile",
        scatter_dimension=0,
        tiled=True,
    ).astype(jnp.float32)
    return (summed_out + bias_out).astype(jnp.bfloat16)


def layer_kernel(
    groups,
    ids_hbm, deg_hbm, feats_hbm, table_hbm, win_hbm, bin_hbm, wout_hbm, bout_hbm,
    out_ref,
    ids_raw, deg_raw, bin_ref, bout_ref, ids_ref, deg_row, deg_col,
    table, win, wout, feats_own, idbuf, keys, rowkeys, count,
    sum_a, sum_b, rx, own_sum, zsend, zrecv, feats_all, agg_all, part, pouts, prx, qsend, qrx,
    ldsem, tsem, idsem_s, idsem_r, rs_s, rs_r, z_s, z_r, fg_s, fg_r, ag_s, ag_r, pp_s, pp_r, q_s, q_r,
):
    f32, bf16 = jnp.float32, jnp.bfloat16
    g = lax.axis_index("grp")
    t = lax.axis_index("tile")
    c = lax.rem(t, 2)
    x = lax.rem(t // 2, 2)
    y = t // 4
    rows, width = table_hbm.shape
    nodes = feats_hbm.shape[0]
    half = width // 2
    slots = ids_hbm.shape[0]

    def dev(dg, rel, dc=0):
        xx = lax.rem(x + rel % 2, 2)
        yy = lax.rem(y + rel // 2, 2)
        cc = lax.rem(c + dc, 2)
        return (lax.rem(g + dg, groups), (yy * 2 + xx) * 2 + cc)

    def remote(src, dst, ss, rs, where):
        return pltpu.make_async_remote_copy(
            src_ref=src, dst_ref=dst, send_sem=ss, recv_sem=rs, device_id=where, device_id_type=MESH
        )

    mine = pl.ds(pl.multiple_of(c * rows, rows), rows)
    loads = [
        pltpu.make_async_copy(table_hbm, table.at[mine], ldsem.at[0]),
        pltpu.make_async_copy(feats_hbm, feats_all.at[0, 0], ldsem.at[1]),
        pltpu.make_async_copy(win_hbm, win, ldsem.at[2]),
        pltpu.make_async_copy(wout_hbm, wout, ldsem.at[3]),
        pltpu.make_async_copy(feats_hbm, feats_own, ldsem.at[4]),
        pltpu.make_async_copy(ids_hbm, ids_raw, ldsem.at[5]),
        pltpu.make_async_copy(deg_hbm, deg_raw, ldsem.at[6]),
        pltpu.make_async_copy(bin_hbm, bin_ref, ldsem.at[7]),
        pltpu.make_async_copy(bout_hbm, bout_ref, ldsem.at[8]),
    ]
    for at in (5, 6, 4, 0, 1, 2, 7, 3, 8):
        loads[at].start()

    barrier = pltpu.get_barrier_semaphore()
    peers = [dev(dg, rel) for dg in range(groups) for rel in range(4) if dg or rel]
    peers.append(dev(0, 0, 1))
    for where in peers:
        pl.semaphore_signal(barrier, inc=1, device_id=where, device_id_type=MESH)

    lane = lax.broadcasted_iota(jnp.int32, (16, 2 * rows), 1)
    rowkeys[...] = jnp.left_shift(lax.rem(lane, LANES) + LANES, lane // LANES).astype(f32).astype(bf16)
    loads[5].wait()
    loads[6].wait()
    degree = deg_raw[...]
    live = lax.broadcasted_iota(jnp.int32, (slots, nodes), 0) < degree
    if nodes < LANES:
        ids_ref[...] = jnp.full((slots, LANES), -1, jnp.int32)
    ids_ref[:, 0:nodes] = jnp.where(live, ids_raw[...], -1)
    idbuf[groups - 1, 0] = ids_ref[...]
    deg_row[...] = jnp.ones((1, LANES), f32)
    deg_row[:, 0:nodes] = degree.astype(f32)

    pl.semaphore_wait(barrier, len(peers))

    id_sends = []
    for i in range(groups):
        for rel in range(4):
            if i == groups - 1 and rel == 0:
                continue
            send = remote(ids_ref, idbuf.at[i, rel], idsem_s.at[i, rel], idsem_r.at[i, rel],
                          dev(groups - 1 - i, rel))
            send.start()
            id_sends.append(send)
    tsend = remote(table_hbm, table.at[mine], tsem.at[0], tsem.at[1], dev(0, 0, 1))
    tsend.start()
    loads[4].wait()
    fsends = []
    for rel in (3, 1, 2):
        send = remote(feats_own, feats_all.at[0, rel], fg_s.at[0, rel], fg_r.at[0, rel], dev(0, rel))
        send.start()
        fsends.append(send)
    send = remote(feats_own, feats_all.at[1, 0], fg_s.at[1, 0], fg_r.at[1, 0], dev(0, 0, 1))
    send.start()
    fsends.append(send)

    deg_col[...] = jnp.broadcast_to(deg_row[...], (LANES, LANES)).T
    for send in id_sends:
        send.wait_recv()
    base = (g * lax.axis_size("tile") + (y * 2 + x) * 2) * rows
    local = idbuf[...].reshape(groups * 4 * slots, LANES) - base
    inside = (local >= 0) & (local < 2 * rows)
    safe = jnp.where(inside, local, 0)
    key = jnp.left_shift(lax.rem(safe, LANES) + LANES, safe // LANES)
    keyf = jnp.where(inside, key, 0).astype(f32)
    if keyf.shape[0] < LANES:
        keyf = jnp.concatenate([keyf, jnp.zeros((LANES - keyf.shape[0], LANES), f32)], axis=0)
    keys[...] = keyf.T

    loads[0].wait()
    tsend.wait_recv()

    def rs_copy(kind, i):
        src = (sum_a.at[i, 3], sum_a.at[i, 1], sum_b.at[i, 3], sum_b.at[i, 2],
               sum_a.at[i, 2], sum_b.at[i, 1])[kind]
        return remote(src, rx.at[kind, i], rs_s.at[kind, i], rs_r.at[kind, i],
                      dev(0, (1, 1, 2, 2, 2, 1)[kind]))

    one = jnp.ones((16, 2 * rows), bf16)
    zero = jnp.zeros((16, 2 * rows), bf16)

    def make_sums(i):
        for rel in range(4):
            block = i * 4 + rel

            def group(r, carry, rel=rel, block=block):
                at = pl.ds(pl.multiple_of(r * 16, 16), 16)
                kk = keys[at, :]
                rk = rowkeys[...]
                total = zero
                for k in range(slots):
                    col = block * slots + k
                    wide = jnp.broadcast_to(kk[:, col:col + 1], (16, LANES)).astype(bf16)
                    wide = jnp.concatenate([wide] * (2 * rows // LANES), axis=1)
                    total = total + jnp.where(wide == rk, one, zero)
                count[pl.ds(pl.multiple_of(rel * nodes + r * 16, 16), 16), :] = total
                return carry

            lax.fori_loop(0, nodes // 16, group, 0)
        step = min(256, half)
        for n0 in range(0, width, step):
            got = jnp.dot(count[...], table[:, n0:n0 + step], preferred_element_type=f32).astype(bf16)
            into, at = (sum_a, n0) if n0 < half else (sum_b, n0 - half)
            into[i, :, :, at:at + step] = got.reshape(4, nodes, step)
            if n0 + step == half:
                rs_copy(0, i).start()
                rs_copy(1, i).start()
        rs_copy(2, i).start()
        rs_copy(3, i).start()

    def pass_on(i):
        rs_copy(0, i).wait_recv()
        sum_a[i, 2] = (sum_a[i, 2].astype(f32) + rx[0, i].astype(f32)).astype(bf16)
        rs_copy(4, i).start()
        rs_copy(2, i).wait_recv()
        sum_b[i, 1] = (sum_b[i, 1].astype(f32) + rx[2, i].astype(f32)).astype(bf16)
        rs_copy(5, i).start()

    def z_copy(i):
        return remote(zsend.at[i], zrecv.at[i], z_s.at[i], z_r.at[i], dev(i + 1, 0))

    def plane_sum(i):
        for kind in (1, 4, 3, 5):
            rs_copy(kind, i).wait_recv()
        a = sum_a[i, 0].astype(f32) + rx[1, i].astype(f32) + rx[4, i].astype(f32)
        b = sum_b[i, 0].astype(f32) + rx[3, i].astype(f32) + rx[5, i].astype(f32)
        if i < groups - 1:
            zsend[i, :, 0:half] = a.astype(bf16)
            zsend[i, :, half:width] = b.astype(bf16)
            z_copy(i).start()
        else:
            own_sum[:, 0:half] = a
            own_sum[:, half:width] = b

    def gather_copy(buf, ss, rs, kind, rel):
        if kind == 0:
            return remote(buf.at[0, 0], buf.at[0, rel], ss.at[0, rel], rs.at[0, rel], dev(0, rel))
        return remote(buf.at[0, rel], buf.at[1, rel], ss.at[1, rel], rs.at[1, rel], dev(0, 0, 1))

    make_sums(0)
    make_sums(1)
    loads[1].wait()
    for rel in (1, 2, 3):
        gather_copy(feats_all, fg_s, fg_r, 0, rel).wait_recv()
        gather_copy(feats_all, fg_s, fg_r, 1, rel).start()
    pass_on(0)
    for i in range(2, groups):
        make_sums(i)
        pass_on(i - 1)
        plane_sum(i - 2)

    loads[2].wait()
    loads[7].wait()
    for rel in range(4):
        gather_copy(feats_all, fg_s, fg_r, 1, rel).wait_recv()
    hid = win.shape[1]

    part[...] = jnp.dot(
        feats_all[...].reshape(8 * nodes, width), win[0:width, :], preferred_element_type=f32
    ).reshape(2, 4, nodes, hid) + bin_ref[...].reshape(1, 1, 1, hid)

    plane_sum(groups - 2)
    pass_on(groups - 1)
    plane_sum(groups - 1)

    total = own_sum[...]
    for i in range(groups - 1):
        z_copy(i).wait_recv()
        total = total + zrecv[i].astype(f32)
    divisor = jnp.concatenate([deg_col[0:nodes, :]] * (width // LANES), axis=1)
    agg_all[0, 0] = (total / divisor).astype(bf16)
    for rel in (1, 2, 3):
        gather_copy(agg_all, ag_s, ag_r, 0, rel).start()
    gather_copy(agg_all, ag_s, ag_r, 1, 0).start()
    loads[3].wait()
    loads[8].wait()

    def p_copy(rel):
        return remote(pouts.at[1, rel], prx.at[rel], pp_s.at[rel], pp_r.at[rel], dev(0, 0, 1))

    def q_copy(rel):
        return remote(qsend.at[rel - 1], qrx.at[rel - 1], q_s.at[rel - 1], q_r.at[rel - 1], dev(0, rel))

    def forward(rel):
        gather_copy(agg_all, ag_s, ag_r, 0, rel).wait_recv()
        gather_copy(agg_all, ag_s, ag_r, 1, rel).start()

    def block(rel):
        gather_copy(agg_all, ag_s, ag_r, 1, rel).wait_recv()
        both = agg_all[:, rel].reshape(2 * nodes, width)
        pre = jnp.dot(both, win[width:2 * width, :], preferred_element_type=f32)
        pre = pre + part[:, rel].reshape(2 * nodes, hid)
        hidden = jnp.maximum(pre, 0.0).astype(bf16)
        got = jnp.dot(hidden, wout[...], preferred_element_type=f32).astype(bf16)
        pouts[:, rel] = got.reshape(2, nodes, got.shape[1])
        p_copy(rel).start()

    def send_out(rel):
        p_copy(rel).wait_recv()
        qsend[rel - 1] = (pouts[0, rel].astype(f32) + prx[rel].astype(f32)).astype(bf16)
        q_copy(rel).start()

    block(0)
    forward(1)
    forward(2)
    block(1)
    forward(3)
    block(2)
    send_out(1)
    block(3)
    send_out(2)
    send_out(3)
    p_copy(0).wait_recv()
    final = pouts[0, 0].astype(f32) + prx[0].astype(f32) + bout_ref[...]
    for rel in (1, 2, 3):
        q_copy(rel).wait_recv()
        final = final + qrx[rel - 1].astype(f32)
    out_ref[...] = final.astype(bf16)

    for send in id_sends + fsends:
        send.wait_send()
    tsend.wait_send()
    for rel in (1, 2, 3):
        gather_copy(feats_all, fg_s, fg_r, 1, rel).wait_send()
        gather_copy(agg_all, ag_s, ag_r, 0, rel).wait_send()
        q_copy(rel).wait_send()
    for rel in range(4):
        gather_copy(agg_all, ag_s, ag_r, 1, rel).wait_send()
        p_copy(rel).wait_send()
    for i in range(groups):
        for kind in range(6):
            rs_copy(kind, i).wait_send()
        if i < groups - 1:
            z_copy(i).wait_send()


def on_device_fused(groups, node_feats, feature_table, nbr_ids, degree, weight_in, bias_in, weight_out, bias_out):
    nodes, slots = nbr_ids.shape
    rows, width = feature_table.shape
    hid = weight_in.shape[1]
    outw = weight_out.shape[1]
    bf16, f32 = jnp.bfloat16, jnp.float32
    vmem = pl.BlockSpec(memory_space=pltpu.VMEM)
    hbm = pl.BlockSpec(memory_space=pltpu.HBM)
    half = width // 2
    dma = pltpu.SemaphoreType.DMA
    return pl.pallas_call(
        functools.partial(layer_kernel, groups),
        out_shape=jax.ShapeDtypeStruct((nodes, outw), bf16),
        in_specs=[hbm] * 8,
        out_specs=vmem,
        scratch_shapes=[
            pltpu.VMEM((slots, nodes), jnp.int32),
            pltpu.VMEM((1, nodes), jnp.int32),
            pltpu.VMEM((1, hid), f32),
            pltpu.VMEM((1, outw), f32),
            pltpu.VMEM((slots, LANES), jnp.int32),
            pltpu.VMEM((1, LANES), f32),
            pltpu.VMEM((LANES, LANES), f32),
            pltpu.VMEM((2 * rows, width), bf16),
            pltpu.VMEM((2 * width, hid), bf16),
            pltpu.VMEM((hid, outw), bf16),
            pltpu.VMEM((nodes, width), bf16),
            pltpu.VMEM((groups, 4, slots, LANES), jnp.int32),
            pltpu.VMEM((LANES, LANES), f32),
            pltpu.VMEM((16, 2 * rows), bf16),
            pltpu.VMEM((4 * nodes, 2 * rows), bf16),
            pltpu.VMEM((groups, 4, nodes, half), bf16),
            pltpu.VMEM((groups, 4, nodes, half), bf16),
            pltpu.VMEM((6, groups, nodes, half), bf16),
            pltpu.VMEM((nodes, width), f32),
            pltpu.VMEM((groups - 1, nodes, width), bf16),
            pltpu.VMEM((groups - 1, nodes, width), bf16),
            pltpu.VMEM((2, 4, nodes, width), bf16),
            pltpu.VMEM((2, 4, nodes, width), bf16),
            pltpu.VMEM((2, 4, nodes, hid), f32),
            pltpu.VMEM((2, 4, nodes, outw), bf16),
            pltpu.VMEM((4, nodes, outw), bf16),
            pltpu.VMEM((3, nodes, outw), bf16),
            pltpu.VMEM((3, nodes, outw), bf16),
            dma((9,)), dma((2,)),
            dma((groups, 4)), dma((groups, 4)),
            dma((6, groups)), dma((6, groups)),
            dma((groups - 1,)), dma((groups - 1,)),
            dma((2, 4)), dma((2, 4)),
            dma((2, 4)), dma((2, 4)),
            dma((4,)), dma((4,)),
            dma((3,)), dma((3,)),
        ],
        compiler_params=pltpu.CompilerParams(
            collective_id=0, has_side_effects=True, vmem_limit_bytes=67043328
        ),
    )(
        nbr_ids.T, degree[None, :], node_feats, feature_table, weight_in,
        bias_in[None, :], weight_out, bias_out[None, :],
    )


def solution(mesh):
    groups, tiles = mesh.shape["grp"], mesh.shape["tile"]

    def on_device(node_feats, feature_table, nbr_ids, degree, *weights):
        nodes, slots = nbr_ids.shape
        rows, width = feature_table.shape
        fits = (
            tiles == 8
            and groups > 2
            and groups * 4 * slots <= LANES
            and nodes <= LANES
            and nodes % 16 == 0
            and rows % LANES == 0
            and 2 * rows // LANES <= 16
            and width % (4 * LANES) == 0
        )
        if fits:
            return on_device_fused(groups, node_feats, feature_table, nbr_ids, degree, *weights)
        return on_device_xla(node_feats, feature_table, nbr_ids, degree, *weights)

    return jax.shard_map(
        on_device,
        mesh=mesh,
        in_specs=(
            P(("grp", "tile"), None),
            P(("grp", "tile"), None),
            P(("grp", "tile"), None),
            P(("grp", "tile")),
            P(None, "tile"),
            P("tile"),
            P("tile", None),
            P(),
        ),
        out_specs=P(("grp", "tile"), None),
        check_vma=False,
    )
```
